32 devices in a mesh: clips: 2 (over y), pix: 4 (over z), pair: 2 (over x), dir: 2 (over core).
Axes of the slice: x: 2, y: 2, z: 4, core: 2. Of those that a mesh axis runs over, the one named last changes fastest.
Arguments:
- features: bfloat16 [4, 2, 1920, 128], P(('clips', 'pair'), 'dir', 'pix'), parts along dimension 0, may hold values from -6 to 6
Outputs:
- flow: float32 [4, 2, 2, 1920], P(('clips', 'pair'), 'dir', None, 'pix'), parts along dimension 0
- matched: bfloat16 [4, 2, 1920, 128], P(('clips', 'pair'), 'dir', 'pix'), parts along dimension 0
The draws below stay inside these ranges and needn't reach their ends.
There are 2 independent parts, one for each index of `clips`. The reference program is written for one: setup_inputs(seed, part) draws one part's arguments, and reference() takes and returns one part's arrays. A program takes and returns all parts, laid end to end along the dimension named above; each array names one. Nothing has to cross between parts.
All inputs are finite; a program needn't handle non-finite values.
Results may differ from the reference program's by a relative error of at most 0.0065.
Values may be sent and summed in bfloat16 or wider, within the bound.
No kernel may reach another device: no remote copies, remote signals or barrier semaphores. Data moves between devices by JAX's collectives and lax.ppermute only.
A program may use at most 64 MiB of HBM per device.

```python
import jax
import jax.numpy as jnp
from jax import lax

C = 128
W = 120
ROWS_DEV = 4
PIXELS = 1920
PAIRS = 2


def draw_features(key, part):
    keys = jax.random.split(key, 1)
    shape = (PAIRS, 2, PIXELS, C)
    base = jnp.clip(1.75 * jax.random.normal(keys[0], shape, jnp.float32), -6.0, 6.0)
    return base.astype(jnp.bfloat16)


def setup_inputs(seed: int = 0, part: int = 0) -> dict:
    seeds = jax.random.split(jax.random.key(seed), 2)
    part_splits = jax.random.split(jax.random.fold_in(seeds[1], part), 2)
    return {
        "features": draw_features(jax.random.fold_in(jax.random.fold_in(seeds[1], part), 71), part),
    }


def match_block(queries, targets, posx, posy, own_x, own_y):
    scores = jnp.dot(queries, targets.T, preferred_element_type=jnp.float32) * (C ** -0.5)
    top = jnp.max(scores, axis=1, keepdims=True)
    weights = jnp.exp(scores - top)
    total = jnp.sum(weights, axis=1)
    flow_x = jnp.sum(weights * posx[None, :], axis=1) / total - own_x
    flow_y = jnp.sum(weights * posy[None, :], axis=1) / total - own_y
    rounded = weights.astype(jnp.bfloat16)
    summed = jnp.dot(rounded, targets, preferred_element_type=jnp.float32)
    matched = (summed / total[:, None]).astype(jnp.bfloat16)
    return jnp.stack([flow_x, flow_y]), matched


def reference(features):
    index = jnp.arange(PIXELS, dtype=jnp.int32)
    posx = (index % W).astype(jnp.float32) / W
    posy = (index // W).astype(jnp.float32) / W
    block = ROWS_DEV * W
    count = PIXELS // block
    flows = []
    matches = []
    for pair_index in range(PAIRS):
        flow_dirs = []
        match_dirs = []
        for side in range(2):
            sources = features[pair_index, side].reshape(count, block, C)
            targets = features[pair_index, 1 - side]
            own_x = posx.reshape(count, block)
            own_y = posy.reshape(count, block)

            def one_block(item):
                return match_block(item[0], targets, posx, posy, item[1], item[2])

            flow_part, match_part = lax.map(one_block, (sources, own_x, own_y))
            flow_dirs.append(jnp.transpose(flow_part, (1, 0, 2)).reshape(2, PIXELS))
            match_dirs.append(match_part.reshape(PIXELS, C))
        flows.append(jnp.stack(flow_dirs))
        matches.append(jnp.stack(match_dirs))
    return jnp.stack(flows), jnp.stack(matches)
```

```python
import functools
import math

import jax
import jax.numpy as jnp
from jax import lax
from jax.experimental import pallas as pl
from jax.experimental.pallas import tpu as pltpu
from jax.sharding import PartitionSpec as P

W = 120
FORWARD = 0.0
VMEM = pl.BlockSpec(memory_space=pltpu.VMEM)


def hop(array, shift, cross):
    pix, frames = lax.axis_size("pix"), lax.axis_size("dir")
    flip = 1 if cross else 0
    pairs = [
        (z * frames + d, (z ^ shift) * frames + (d ^ flip)) for z in range(pix) for d in range(frames)
    ]
    return lax.ppermute(array, ("pix", "dir"), pairs)


def local_positions(rows, chans):
    column = lax.broadcasted_iota(jnp.int32, (rows, chans), 1)
    index = lax.broadcasted_iota(jnp.int32, (rows, chans), 0).astype(jnp.float32)
    row = jnp.floor((index + 0.5) * (1.0 / W))
    place = index - row * W
    values = jnp.where(column == 0, place, jnp.where(column == 1, row, 1.0))
    return jnp.where(column < 3, values, 0.0).astype(jnp.bfloat16)


def fold_kernel(shifts, counts, first, last, rows_here, *refs):
    refs = list(refs)
    q_ref = refs.pop(0)
    key_refs = [[refs.pop(0) for _ in range(n)] for n in counts]
    if not first:
        top_in, acc_in, pos_in = refs.pop(0), refs.pop(0), refs.pop(0)
        pos = pos_in[...]
    else:
        pos = local_positions(rows_here, q_ref.shape[1])
    queries = q_ref[...]
    chans = queries.shape[1]
    scale = chans ** (-0.5) * math.log2(math.e)
    here = lax.axis_index("pix")
    column = lax.broadcasted_iota(jnp.int32, (1, chans), 1)
    keys, values = [], []
    for shift, block in zip(shifts, key_refs):
        part = jnp.concatenate([ref[...] for ref in block], axis=0) if len(block) > 1 else block[0][...]
        start_row = (here ^ shift) * (rows_here // W)
        offset = jnp.where(column == 1, start_row, 0).astype(jnp.float32).astype(jnp.bfloat16)
        keys.append(part)
        values.append(jnp.concatenate([part, pos + offset], axis=1))
    keys = jnp.concatenate(keys, axis=0) if len(keys) > 1 else keys[0]
    values = jnp.concatenate(values, axis=0) if len(values) > 1 else values[0]
    scores = lax.dot_general(queries, keys, (((1,), (1,)), ((), ())), preferred_element_type=jnp.float32)
    top = jnp.max(scores, axis=1, keepdims=True)
    if not first:
        old = top_in[...]
        top = jnp.maximum(old[:, :1], top)
    weights = jnp.exp2((scores - top) * scale).astype(jnp.bfloat16)
    acc = jnp.dot(weights, values, preferred_element_type=jnp.float32)
    if not first:
        acc = acc + acc_in[...] * jnp.exp2((old[:, :1] - top) * scale)
    if not last:
        top_out, acc_out = refs.pop(0), refs.pop(0)
        top_out[...] = jnp.broadcast_to(top, top_out.shape)
        acc_out[...] = acc
        if first:
            refs.pop(0)[...] = pos
        return
    flow_ref, matched_ref = refs
    inverse = 1.0 / acc[:, chans + 2 : chans + 3]
    matched_ref[...] = (acc[:, :chans] * inverse).astype(jnp.bfloat16)
    sums = jnp.transpose(acc[:, chans:] * inverse)[:2, :]
    index = (here * rows_here + lax.broadcasted_iota(jnp.int32, (1, rows_here), 1)).astype(jnp.float32)
    own_row = jnp.floor((index + 0.5) * (1.0 / W))
    own_place = index - own_row * W
    flow_ref[...] = (sums - jnp.concatenate([own_place, own_row], axis=0)) * (1.0 / W)


def fold(queries, blocks, carry, last):
    rows, chans = queries.shape
    shifts = [shift for shift, _ in blocks]
    counts = [len(parts) for _, parts in blocks]
    first = carry is None
    if last:
        shapes = ((2, rows), jnp.float32), ((rows, chans), jnp.bfloat16)
    else:
        shapes = ((rows, chans), jnp.float32), ((rows, 2 * chans), jnp.float32)
        if first:
            shapes += (((rows, chans), jnp.bfloat16),)
    operands = [queries] + [part for _, parts in blocks for part in parts] + list(carry or ())
    keys = sum(part.shape[0] for _, parts in blocks for part in parts)
    outs = pl.pallas_call(
        functools.partial(fold_kernel, shifts, counts, first, last, rows),
        out_shape=[jax.ShapeDtypeStruct(shape, kind) for shape, kind in shapes],
        in_specs=[VMEM] * len(operands),
        out_specs=[VMEM] * len(shapes),
        compiler_params=pltpu.CompilerParams(vmem_limit_bytes=24 * 1024 * 1024),
        cost_estimate=pl.CostEstimate(
            flops=6 * rows * keys * chans, bytes_accessed=2 * keys * chans, transcendentals=rows * keys
        ),
    )(*operands)
    if last:
        return outs
    return (outs[0], outs[1], outs[2] if first else carry[2])


def body(features):
    rows, chans = features.shape[2:]
    pix = lax.axis_size("pix")
    cut = int(rows * FORWARD) // 32 * 32
    own = features.reshape(rows, chans)
    blocks = {}
    for far in range(2, pix, 2):
        blocks[far] = hop(own, far, True)
        odd = hop(own[cut:], far ^ 1, True)
        if cut:
            odd = (hop(blocks[far][:cut], 1, False), odd)
        blocks[far ^ 1] = odd if cut else (odd,)
        blocks[far] = (blocks[far],)
    blocks[1] = (hop(own, 1, True),)
    blocks[0] = (hop(own, 0, True),)
    groups = [[0], [1]] + [[far, far ^ 1][i : i + 1] for far in range(2, pix, 2) for i in range(2)]
    carry = None
    for group in groups:
        carry = fold(own, [(s, blocks[s]) for s in group], carry, group is groups[-1])
    flow, matched = carry
    return flow.reshape(1, 1, 2, rows), matched.reshape(1, 1, rows, chans)


def solution(mesh):
    return jax.shard_map(
        body,
        mesh=mesh,
        in_specs=(P(("clips", "pair"), "dir", "pix", None),),
        out_specs=(
            P(("clips", "pair"), "dir", None, "pix"),
            P(("clips", "pair"), "dir", "pix", None),
        ),
        check_vma=False,
    )
```

```python
import functools
import math

import jax
import jax.numpy as jnp
from jax import lax
from jax.experimental import pallas as pl
from jax.experimental.pallas import tpu as pltpu
from jax.sharding import PartitionSpec as P

W = 120
VMEM = pl.BlockSpec(memory_space=pltpu.VMEM)
ANY = pl.BlockSpec(memory_space=pl.ANY)
PARAMS = pltpu.CompilerParams(vmem_limit_bytes=24 * 1024 * 1024)


def hop(array, targets, cross):
    frames = lax.axis_size("dir")
    flip = 1 if cross else 0
    pairs = [
        (z * frames + d, t * frames + (d ^ flip))
        for z, t in enumerate(targets)
        if t is not None
        for d in range(frames)
    ]
    return lax.ppermute(array, ("pix", "dir"), pairs)


def pick(table):
    here = lax.axis_index("pix")
    value = jnp.int32(0)
    for z, entry in enumerate(table):
        value = jnp.where(here == z, entry, value)
    return value


def places_kernel(out_ref):
    rows, chans = out_ref.shape
    column = lax.broadcasted_iota(jnp.int32, (rows, chans), 1)
    index = lax.broadcasted_iota(jnp.int32, (rows, chans), 0).astype(jnp.float32)
    row = jnp.floor((index + 0.5) * (1.0 / W))
    place = index - row * W
    values = jnp.where(column == 0, place, jnp.where(column == 1, row, 1.0))
    out_ref[...] = jnp.where(column < 3, values, 0.0).astype(jnp.bfloat16)


def places(rows, chans):
    return pl.pallas_call(
        places_kernel,
        out_shape=jax.ShapeDtypeStruct((rows, chans), jnp.bfloat16),
        out_specs=VMEM,
        compiler_params=PARAMS,
        cost_estimate=pl.CostEstimate(flops=rows * chans, bytes_accessed=0, transcendentals=0),
    )()


def fold_kernel(blocks, spans, first, last, *refs):
    refs = list(refs)
    q_ref = refs.pop(0)
    key_refs = [[refs.pop(0) for _ in range(n)] for _, n in blocks]
    places_ref = refs.pop(0)
    if not first:
        top_in, acc_in = refs.pop(0), refs.pop(0)
    rows, chans = q_ref.shape
    scale = chans ** (-0.5) * math.log2(math.e)
    here = lax.axis_index("pix")
    column = lax.broadcasted_iota(jnp.int32, (1, chans), 1)
    keys, values = [], []
    for (table, _), held in zip(blocks, key_refs):
        part = held[0][...]
        if len(held) > 1:
            part = jnp.where((here == 0) | (here == len(table) - 1), held[1][...], part)
        start_row = pick(table) * (part.shape[0] // W)
        offset = jnp.where(column == 1, start_row, 0).astype(jnp.float32).astype(jnp.bfloat16)
        keys.append(part)
        values.append(jnp.concatenate([part, places_ref[...] + offset], axis=1))
    keys = jnp.concatenate(keys, axis=0) if len(keys) > 1 else keys[0]
    values = jnp.concatenate(values, axis=0) if len(values) > 1 else values[0]
    count = keys.shape[0]
    scores = [
        lax.dot_general(
            q_ref[begin:end, :], keys, (((1,), (1,)), ((), ())), preferred_element_type=jnp.float32
        )
        for begin, end in spans
    ]
    tops, fades, weights = [], [], []
    for score, (begin, end) in zip(scores, spans):
        top = jnp.broadcast_to(jnp.max(score, axis=1, keepdims=True), (end - begin, chans))
        if not first:
            old = top_in[begin:end, :]
            top = jnp.maximum(old, top)
            fades.append(jnp.exp2((old - top) * scale))
        tops.append(top)
        parts = [
            jnp.exp2((score[:, j : j + chans] - top[:, : min(chans, count - j)]) * scale).astype(jnp.bfloat16)
            for j in range(0, count, chans)
        ]
        weights.append(jnp.concatenate(parts, axis=1) if len(parts) > 1 else parts[0])
    accs = [jnp.dot(weight, values, preferred_element_type=jnp.float32) for weight in weights]
    if not first:
        accs = [
            acc + acc_in[begin:end, :] * jnp.concatenate([fade, fade], axis=1)
            for acc, fade, (begin, end) in zip(accs, fades, spans)
        ]
    if not last:
        top_out, acc_out = refs
        for acc, top, (begin, end) in zip(accs, tops, spans):
            top_out[begin:end, :] = top
            acc_out[begin:end, :] = acc
        return
    flow_hbm, matched_hbm, flow_ref, matched_ref, sems = refs
    copies = []
    for place, (acc, (begin, end)) in enumerate(zip(accs, spans)):
        inverse = 1.0 / acc[:, chans + 2 : chans + 3]
        matched_ref[begin:end, :] = (acc[:, :chans] * inverse).astype(jnp.bfloat16)
        copies.append(
            pltpu.make_async_copy(
                matched_ref.at[begin:end, :], matched_hbm.at[begin:end, :], sems.at[place]
            )
        )
        copies[-1].start()
        sums = jnp.transpose(acc[:, chans:] * inverse)[:2, :]
        index = here * rows + begin + lax.broadcasted_iota(jnp.int32, (1, end - begin), 1)
        index = index.astype(jnp.float32)
        own_row = jnp.floor((index + 0.5) * (1.0 / W))
        own = jnp.concatenate([index - own_row * W, own_row], axis=0)
        flow_ref[:, begin:end] = (sums - own) * (1.0 / W)
    copies.append(pltpu.make_async_copy(flow_ref, flow_hbm, sems.at[len(spans)]))
    copies[-1].start()
    for copy in copies:
        copy.wait()


def fold(queries, positions, blocks, carry, last):
    rows, chans = queries.shape
    first = carry is None
    middle = (rows // 2 + 127) // 128 * 128
    spans = [(0, middle), (middle, rows)] if middle < rows else [(0, rows)]
    operands = [queries, *[part for _, held in blocks for part in held], positions, *(carry or ())]
    keys = sum(held[0].shape[0] for _, held in blocks)
    if last:
        shapes = ((2, rows), jnp.float32), ((rows, chans), jnp.bfloat16)
        scratch = [pltpu.VMEM(shape, kind) for shape, kind in shapes]
        scratch.append(pltpu.SemaphoreType.DMA((len(spans) + 1,)))
    else:
        shapes = ((rows, chans), jnp.float32), ((rows, 2 * chans), jnp.float32)
        scratch = []
    return pl.pallas_call(
        functools.partial(fold_kernel, [(table, len(held)) for table, held in blocks], spans, first, last),
        out_shape=[jax.ShapeDtypeStruct(shape, kind) for shape, kind in shapes],
        in_specs=[VMEM] * len(operands),
        out_specs=[ANY if last else VMEM] * len(shapes),
        scratch_shapes=scratch,
        compiler_params=PARAMS,
        cost_estimate=pl.CostEstimate(
            flops=6 * rows * keys * chans, bytes_accessed=2 * keys * chans, transcendentals=rows * keys
        ),
    )(*operands)


def sources_of(targets):
    return [targets.index(z) for z in range(len(targets))]


def body(features):
    rows, chans = features.shape[2:]
    pix = lax.axis_size("pix")
    straight = list(range(pix))
    own = features.reshape(rows, chans)

    def send(array, targets, cross=True):
        return hop(array, targets, cross)

    positions = places(rows, chans)
    if pix == 4:
        far = send(own, [2, 0, 3, 1])
        back = send(own, [1, 3, 0, 2])
        zero = send(own, straight)
        mid = send(own, [0, 2, 1, 3])
        relay = send(far, [1, 0, 3, 2], False)
        groups = [
            [(straight, [zero])],
            [(sources_of([2, 0, 3, 1]), [far])],
            [(sources_of([1, 3, 0, 2]), [back])],
            [(straight[::-1], [mid, relay])],
        ]
    else:
        groups = []
        for shift in range(pix):
            targets = [(z + shift) % pix for z in range(pix)]
            groups.append([(sources_of(targets), [send(own, targets)])])
    carry = None
    for place, blocks in enumerate(groups):
        carry = fold(own, positions, blocks, carry, place == len(groups) - 1)
    flow, matched = carry
    return flow.reshape(1, 1, 2, rows), matched.reshape(1, 1, rows, chans)


def solution(mesh):
    return jax.shard_map(
        body,
        mesh=mesh,
        in_specs=(P(("clips", "pair"), "dir", "pix", None),),
        out_specs=(
            P(("clips", "pair"), "dir", None, "pix"),
            P(("clips", "pair"), "dir", "pix", None),
        ),
        check_vma=False,
    )
```

```python
import functools
import math

import jax
import jax.numpy as jnp
from jax import lax
from jax.experimental import pallas as pl
from jax.experimental.pallas import tpu as pltpu
from jax.sharding import PartitionSpec as P

W = 120
VMEM = pl.BlockSpec(memory_space=pltpu.VMEM)
ANY = pl.BlockSpec(memory_space=pl.ANY)
PARAMS = pltpu.CompilerParams(vmem_limit_bytes=24 * 1024 * 1024)


def hop(array, targets, cross):
    frames = lax.axis_size("dir")
    flip = 1 if cross else 0
    pairs = [
        (z * frames + d, t * frames + (d ^ flip))
        for z, t in enumerate(targets)
        if t is not None
        for d in range(frames)
    ]
    return lax.ppermute(array, ("pix", "dir"), pairs)


def pick(table):
    here = lax.axis_index("pix")
    value = jnp.int32(0)
    for z, entry in enumerate(table):
        value = jnp.where(here == z, entry, value)
    return value


def prepare_kernel(own_ref, whole_ref, places_ref, *part_refs):
    whole_ref[...] = own_ref[...]
    begin = 0
    for ref in part_refs:
        ref[...] = own_ref[begin : begin + ref.shape[0], :]
        begin += ref.shape[0]
    rows, chans = places_ref.shape
    column = lax.broadcasted_iota(jnp.int32, (rows, chans), 1)
    index = lax.broadcasted_iota(jnp.int32, (rows, chans), 0).astype(jnp.float32)
    row = jnp.floor((index + 0.5) * (1.0 / W))
    place = index - row * W
    values = jnp.where(column == 0, place, jnp.where(column == 1, row, 1.0))
    places_ref[...] = jnp.where(column < 3, values, 0.0).astype(jnp.bfloat16)


def prepare(own, sizes):
    rows, chans = own.shape
    return pl.pallas_call(
        prepare_kernel,
        out_shape=[jax.ShapeDtypeStruct((size, chans), own.dtype) for size in (rows, rows, *sizes)],
        in_specs=[VMEM],
        out_specs=[VMEM] * (2 + len(sizes)),
        compiler_params=PARAMS,
        cost_estimate=pl.CostEstimate(flops=rows * chans, bytes_accessed=4 * own.size, transcendentals=0),
    )(own)


def fold_kernel(blocks, spans, first, last, *refs):
    refs = list(refs)
    q_ref = refs.pop(0)
    key_refs = [[refs.pop(0) for _ in range(n)] for _, _, n in blocks]
    places_ref = refs.pop(0)
    if not first:
        top_in, acc_in = refs.pop(0), refs.pop(0)
    rows, chans = q_ref.shape
    scale = chans ** (-0.5) * math.log2(math.e)
    here = lax.axis_index("pix")
    column = lax.broadcasted_iota(jnp.int32, (1, chans), 1)
    keys, values = [], []
    for (table, begin, _), held in zip(blocks, key_refs):
        part = held[0][...]
        if len(held) > 1:
            part = jnp.where((here == 0) | (here == len(table) - 1), held[1][...], part)
        start_row = pick(table) * (rows // W)
        offset = jnp.where(column == 1, start_row, 0).astype(jnp.float32).astype(jnp.bfloat16)
        keys.append(part)
        place = places_ref[begin : begin + part.shape[0], :]
        values.append(jnp.concatenate([part, place + offset], axis=1))
    keys = jnp.concatenate(keys, axis=0) if len(keys) > 1 else keys[0]
    values = jnp.concatenate(values, axis=0) if len(values) > 1 else values[0]
    count = keys.shape[0]
    scores = [
        lax.dot_general(
            q_ref[begin:end, :], keys, (((1,), (1,)), ((), ())), preferred_element_type=jnp.float32
        )
        for begin, end in spans
    ]
    tops, fades, weights = [], [], []
    for score, (begin, end) in zip(scores, spans):
        top = jnp.broadcast_to(jnp.max(score, axis=1, keepdims=True), (end - begin, chans))
        if not first:
            old = top_in[begin:end, :]
            top = jnp.maximum(old, top)
            fades.append(jnp.exp2((old - top) * scale))
        tops.append(top)
        parts = [
            jnp.exp2((score[:, j : j + chans] - top[:, : min(chans, count - j)]) * scale).astype(jnp.bfloat16)
            for j in range(0, count, chans)
        ]
        weights.append(jnp.concatenate(parts, axis=1) if len(parts) > 1 else parts[0])
    accs = [jnp.dot(weight, values, preferred_element_type=jnp.float32) for weight in weights]
    if not first:
        accs = [
            acc + acc_in[begin:end, :] * jnp.concatenate([fade, fade], axis=1)
            for acc, fade, (begin, end) in zip(accs, fades, spans)
        ]
    if not last:
        top_out, acc_out = refs
        for acc, top, (begin, end) in zip(accs, tops, spans):
            top_out[begin:end, :] = top
            acc_out[begin:end, :] = acc
        return
    flow_hbm, matched_hbm, flow_ref, matched_ref, sems = refs
    copies = []
    for place, (acc, (begin, end)) in enumerate(zip(accs, spans)):
        inverse = 1.0 / acc[:, chans + 2 : chans + 3]
        matched_ref[begin:end, :] = (acc[:, :chans] * inverse).astype(jnp.bfloat16)
        copies.append(
            pltpu.make_async_copy(
                matched_ref.at[begin:end, :], matched_hbm.at[begin:end, :], sems.at[place]
            )
        )
        copies[-1].start()
        sums = jnp.transpose(acc[:, chans:] * inverse)[:2, :]
        index = here * rows + begin + lax.broadcasted_iota(jnp.int32, (1, end - begin), 1)
        index = index.astype(jnp.float32)
        own_row = jnp.floor((index + 0.5) * (1.0 / W))
        own = jnp.concatenate([index - own_row * W, own_row], axis=0)
        flow_ref[:, begin:end] = (sums - own) * (1.0 / W)
    copies.append(pltpu.make_async_copy(flow_ref, flow_hbm, sems.at[len(spans)]))
    copies[-1].start()
    for copy in copies:
        copy.wait()


def fold(queries, positions, blocks, carry, last):
    rows, chans = queries.shape
    first = carry is None
    middle = (rows // 2 + 127) // 128 * 128
    spans = [(0, middle), (middle, rows)] if middle < rows else [(0, rows)]
    operands = [queries, *[part for _, _, held in blocks for part in held], positions, *(carry or ())]
    keys = sum(held[0].shape[0] for _, _, held in blocks)
    if last:
        shapes = ((2, rows), jnp.float32), ((rows, chans), jnp.bfloat16)
        scratch = [pltpu.VMEM(shape, kind) for shape, kind in shapes]
        scratch.append(pltpu.SemaphoreType.DMA((len(spans) + 1,)))
    else:
        shapes = ((rows, chans), jnp.float32), ((rows, 2 * chans), jnp.float32)
        scratch = []
    return pl.pallas_call(
        functools.partial(fold_kernel, [(table, begin, len(held)) for table, begin, held in blocks], spans, first, last),
        out_shape=[jax.ShapeDtypeStruct(shape, kind) for shape, kind in shapes],
        in_specs=[VMEM] * len(operands),
        out_specs=[ANY if last else VMEM] * len(shapes),
        scratch_shapes=scratch,
        compiler_params=PARAMS,
        cost_estimate=pl.CostEstimate(
            flops=6 * rows * keys * chans, bytes_accessed=2 * keys * chans, transcendentals=rows * keys
        ),
    )(*operands)


def sources_of(targets):
    return [targets.index(z) for z in range(len(targets))]


def body(features):
    rows, chans = features.shape[2:]
    pix = lax.axis_size("pix")
    straight = list(range(pix))
    own = features.reshape(rows, chans)

    def send(array, targets, cross=True):
        return hop(array, targets, cross)

    cut = rows * 8 // 240 * 16
    queries, positions, head, tail = prepare(own, (cut, rows - cut))
    if pix == 4:
        far = send(own, [2, 0, 3, 1])
        back = send(own, [1, 3, 0, 2])
        cross = send(tail, [3, 2, 1, 0])
        zero = send(own, straight)
        mid = send(head, [0, 2, 1, 3])
        relay = send(far[:cut], [1, 0, 3, 2], False)
        groups = [
            [(straight, 0, [zero])],
            [(sources_of([2, 0, 3, 1]), 0, [far])],
            [(sources_of([1, 3, 0, 2]), 0, [back])],
            [(straight[::-1], cut, [cross])],
            [(straight[::-1], 0, [mid, relay])],
        ]
    else:
        groups = []
        for shift in range(pix):
            targets = [(z + shift) % pix for z in range(pix)]
            groups.append([(sources_of(targets), 0, [send(own, targets)])])
    carry = None
    for place, blocks in enumerate(groups):
        carry = fold(queries, positions, blocks, carry, place == len(groups) - 1)
    flow, matched = carry
    return flow.reshape(1, 1, 2, rows), matched.reshape(1, 1, rows, chans)


def solution(mesh):
    return jax.shard_map(
        body,
        mesh=mesh,
        in_specs=(P(("clips", "pair"), "dir", "pix", None),),
        out_specs=(
            P(("clips", "pair"), "dir", None, "pix"),
            P(("clips", "pair"), "dir", "pix", None),
        ),
        check_vma=False,
    )
```

```python
import functools
import math

import jax
import jax.numpy as jnp
from jax import lax
from jax.experimental import pallas as pl
from jax.experimental.pallas import tpu as pltpu
from jax.sharding import PartitionSpec as P

W = 120
VMEM = pl.BlockSpec(memory_space=pltpu.VMEM)
ANY = pl.BlockSpec(memory_space=pl.ANY)
PARAMS = pltpu.CompilerParams(vmem_limit_bytes=24 * 1024 * 1024)


def hop(array, targets, cross):
    frames = lax.axis_size("dir")
    flip = 1 if cross else 0
    pairs = [
        (z * frames + d, t * frames + (d ^ flip))
        for z, t in enumerate(targets)
        if t is not None
        for d in range(frames)
    ]
    return lax.ppermute(array, ("pix", "dir"), pairs)


def pick(table):
    here = lax.axis_index("pix")
    value = jnp.int32(0)
    for z, entry in enumerate(table):
        value = jnp.where(here == z, entry, value)
    return value


def places_kernel(out_ref):
    rows, chans = out_ref.shape
    column = lax.broadcasted_iota(jnp.int32, (rows, chans), 1)
    index = lax.broadcasted_iota(jnp.int32, (rows, chans), 0).astype(jnp.float32)
    row = jnp.floor((index + 0.5) * (1.0 / W))
    place = index - row * W
    values = jnp.where(column == 0, place, jnp.where(column == 1, row, 1.0))
    out_ref[...] = jnp.where(column < 3, values, 0.0).astype(jnp.bfloat16)


def places(rows, chans):
    return pl.pallas_call(
        places_kernel,
        out_shape=jax.ShapeDtypeStruct((rows, chans), jnp.bfloat16),
        out_specs=VMEM,
        compiler_params=PARAMS,
        cost_estimate=pl.CostEstimate(flops=rows * chans, bytes_accessed=0, transcendentals=0),
    )()


def fold_kernel(blocks, spans, first, last, *refs):
    refs = list(refs)
    q_ref = refs.pop(0)
    key_refs = [[refs.pop(0) for _ in range(n)] for _, _, n in blocks]
    places_ref = refs.pop(0)
    if not first:
        top_in, acc_in = refs.pop(0), refs.pop(0)
    rows, chans = q_ref.shape
    scale = chans ** (-0.5) * math.log2(math.e)
    here = lax.axis_index("pix")
    column = lax.broadcasted_iota(jnp.int32, (1, chans), 1)
    keys, values = [], []
    for (table, begin, _), held in zip(blocks, key_refs):
        part = held[0][...]
        if len(held) > 1:
            part = jnp.where((here == 0) | (here == len(table) - 1), held[1][...], part)
        start_row = pick(table) * (rows // W)
        offset = jnp.where(column == 1, start_row, 0).astype(jnp.float32).astype(jnp.bfloat16)
        keys.append(part)
        place = places_ref[begin : begin + part.shape[0], :]
        values.append(jnp.concatenate([part, place + offset], axis=1))
    keys = jnp.concatenate(keys, axis=0) if len(keys) > 1 else keys[0]
    values = jnp.concatenate(values, axis=0) if len(values) > 1 else values[0]
    count = keys.shape[0]
    scores = [
        lax.dot_general(
            q_ref[begin:end, :], keys, (((1,), (1,)), ((), ())), preferred_element_type=jnp.float32
        )
        for begin, end in spans
    ]
    tops, fades, weights = [], [], []
    for score, (begin, end) in zip(scores, spans):
        top = jnp.broadcast_to(jnp.max(score, axis=1, keepdims=True), (end - begin, chans))
        if not first:
            old = top_in[begin:end, :]
            top = jnp.maximum(old, top)
            fades.append(jnp.exp2((old - top) * scale))
        tops.append(top)
        parts = [
            jnp.exp2((score[:, j : j + chans] - top[:, : min(chans, count - j)]) * scale).astype(jnp.bfloat16)
            for j in range(0, count, chans)
        ]
        weights.append(jnp.concatenate(parts, axis=1) if len(parts) > 1 else parts[0])
    accs = [jnp.dot(weight, values, preferred_element_type=jnp.float32) for weight in weights]
    if not first:
        accs = [
            acc + acc_in[begin:end, :] * jnp.concatenate([fade, fade], axis=1)
            for acc, fade, (begin, end) in zip(accs, fades, spans)
        ]
    if not last:
        top_out, acc_out = refs
        for acc, top, (begin, end) in zip(accs, tops, spans):
            top_out[begin:end, :] = top
            acc_out[begin:end, :] = acc
        return
    flow_hbm, matched_hbm, flow_ref, matched_ref, sems = refs
    copies = []
    for place, (acc, (begin, end)) in enumerate(zip(accs, spans)):
        inverse = 1.0 / acc[:, chans + 2 : chans + 3]
        matched_ref[begin:end, :] = (acc[:, :chans] * inverse).astype(jnp.bfloat16)
        copies.append(
            pltpu.make_async_copy(
                matched_ref.at[begin:end, :], matched_hbm.at[begin:end, :], sems.at[place]
            )
        )
        copies[-1].start()
        sums = jnp.transpose(acc[:, chans:] * inverse)[:2, :]
        index = here * rows + begin + lax.broadcasted_iota(jnp.int32, (1, end - begin), 1)
        index = index.astype(jnp.float32)
        own_row = jnp.floor((index + 0.5) * (1.0 / W))
        own = jnp.concatenate([index - own_row * W, own_row], axis=0)
        flow_ref[:, begin:end] = (sums - own) * (1.0 / W)
    copies.append(pltpu.make_async_copy(flow_ref, flow_hbm, sems.at[len(spans)]))
    copies[-1].start()
    for copy in copies:
        copy.wait()


def fold(queries, positions, blocks, carry, last):
    rows, chans = queries.shape
    first = carry is None
    middle = (rows // 2 + 127) // 128 * 128
    spans = [(0, middle), (middle, rows)] if middle < rows else [(0, rows)]
    operands = [queries, *[part for _, _, held in blocks for part in held], positions, *(carry or ())]
    keys = sum(held[0].shape[0] for _, _, held in blocks)
    if last:
        shapes = ((2, rows), jnp.float32), ((rows, chans), jnp.bfloat16)
        scratch = [pltpu.VMEM(shape, kind) for shape, kind in shapes]
        scratch.append(pltpu.SemaphoreType.DMA((len(spans) + 1,)))
    else:
        shapes = ((rows, chans), jnp.float32), ((rows, 2 * chans), jnp.float32)
        scratch = []
    return pl.pallas_call(
        functools.partial(fold_kernel, [(table, begin, len(held)) for table, begin, held in blocks], spans, first, last),
        out_shape=[jax.ShapeDtypeStruct(shape, kind) for shape, kind in shapes],
        in_specs=[VMEM] * len(operands),
        out_specs=[ANY if last else VMEM] * len(shapes),
        scratch_shapes=scratch,
        compiler_params=PARAMS,
        cost_estimate=pl.CostEstimate(
            flops=6 * rows * keys * chans, bytes_accessed=2 * keys * chans, transcendentals=rows * keys
        ),
    )(*operands)


def sources_of(targets):
    return [targets.index(z) for z in range(len(targets))]


def body(features):
    rows, chans = features.shape[2:]
    pix = lax.axis_size("pix")
    own = features.reshape(rows, chans)

    def send(array, targets, cross=True):
        return hop(array, targets, cross)

    positions = places(rows, chans)
    if pix == 4:
        x0 = send(own, [2, 0, 1, 3])
        x1 = send(own, [1, 2, 3, 0])
        x2 = send(own, [0, 3, 2, 1])
        relay = send(x0, [1, 0, 3, 2], False)
        groups = [[(sources_of(t), 0, [x])] for t, x in (([2, 0, 1, 3], x0), ([1, 2, 3, 0], x1), ([0, 3, 2, 1], x2), ([3, 1, 0, 2], relay))]
    else:
        groups = []
        for shift in range(pix):
            targets = [(z + shift) % pix for z in range(pix)]
            groups.append([(sources_of(targets), 0, [send(own, targets)])])
    carry = None
    for place, blocks in enumerate(groups):
        carry = fold(own, positions, blocks, carry, place == len(groups) - 1)
    flow, matched = carry
    return flow.reshape(1, 1, 2, rows), matched.reshape(1, 1, rows, chans)


def solution(mesh):
    return jax.shard_map(
        body,
        mesh=mesh,
        in_specs=(P(("clips", "pair"), "dir", "pix", None),),
        out_specs=(
            P(("clips", "pair"), "dir", None, "pix"),
            P(("clips", "pair"), "dir", "pix", None),
        ),
        check_vma=False,
    )
```

```python
import functools
import math

import jax
import jax.numpy as jnp
from jax import lax
from jax.experimental import pallas as pl
from jax.experimental.pallas import tpu as pltpu
from jax.sharding import PartitionSpec as P

W = 120
VMEM = pl.BlockSpec(memory_space=pltpu.VMEM)
ANY = pl.BlockSpec(memory_space=pl.ANY)
PARAMS = pltpu.CompilerParams(vmem_limit_bytes=24 * 1024 * 1024)


def hop(array, targets, cross):
    frames = lax.axis_size("dir")
    flip = 1 if cross else 0
    pairs = [
        (z * frames + d, t * frames + (d ^ flip))
        for z, t in enumerate(targets)
        if t is not None
        for d in range(frames)
    ]
    return lax.ppermute(array, ("pix", "dir"), pairs)


def pick(table):
    here = lax.axis_index("pix")
    value = jnp.int32(0)
    for z, entry in enumerate(table):
        value = jnp.where(here == z, entry, value)
    return value


def places_kernel(out_ref):
    rows, chans = out_ref.shape
    column = lax.broadcasted_iota(jnp.int32, (rows, chans), 1)
    index = lax.broadcasted_iota(jnp.int32, (rows, chans), 0).astype(jnp.float32)
    row = jnp.floor((index + 0.5) * (1.0 / W))
    place = index - row * W
    values = jnp.where(column == 0, place, jnp.where(column == 1, row, 1.0))
    out_ref[...] = jnp.where(column < 3, values, 0.0).astype(jnp.bfloat16)


def places(rows, chans):
    return pl.pallas_call(
        places_kernel,
        out_shape=jax.ShapeDtypeStruct((rows, chans), jnp.bfloat16),
        out_specs=VMEM,
        compiler_params=PARAMS,
        cost_estimate=pl.CostEstimate(flops=rows * chans, bytes_accessed=0, transcendentals=0),
    )()


def fold_kernel(blocks, spans, first, last, *refs):
    refs = list(refs)
    q_ref = refs.pop(0)
    key_refs = [[refs.pop(0) for _ in range(n)] for _, _, n in blocks]
    places_ref = refs.pop(0)
    if not first:
        top_in, acc_in = refs.pop(0), refs.pop(0)
    rows, chans = q_ref.shape
    scale = chans ** (-0.5) * math.log2(math.e)
    here = lax.axis_index("pix")
    column = lax.broadcasted_iota(jnp.int32, (1, chans), 1)
    keys, values = [], []
    for (table, begin, _), held in zip(blocks, key_refs):
        part = held[0][...]
        if len(held) > 1:
            part = jnp.where((here == 0) | (here == len(table) - 1), held[1][...], part)
        start_row = pick(table) * (rows // W)
        offset = jnp.where(column == 1, start_row, 0).astype(jnp.float32).astype(jnp.bfloat16)
        keys.append(part)
        place = places_ref[begin : begin + part.shape[0], :]
        values.append(jnp.concatenate([part, place + offset], axis=1))
    keys = jnp.concatenate(keys, axis=0) if len(keys) > 1 else keys[0]
    values = jnp.concatenate(values, axis=0) if len(values) > 1 else values[0]
    count = keys.shape[0]
    scores = [
        lax.dot_general(
            q_ref[begin:end, :], keys, (((1,), (1,)), ((), ())), preferred_element_type=jnp.float32
        )
        for begin, end in spans
    ]
    tops, fades, weights = [], [], []
    for score, (begin, end) in zip(scores, spans):
        top = jnp.broadcast_to(jnp.max(score, axis=1, keepdims=True), (end - begin, chans))
        if not first:
            old = top_in[begin:end, :]
            top = jnp.maximum(old, top)
            fades.append(jnp.exp2((old - top) * scale))
        tops.append(top)
        parts = [
            jnp.exp2((score[:, j : j + chans] - top[:, : min(chans, count - j)]) * scale).astype(jnp.bfloat16)
            for j in range(0, count, chans)
        ]
        weights.append(jnp.concatenate(parts, axis=1) if len(parts) > 1 else parts[0])
    accs = [jnp.dot(weight, values, preferred_element_type=jnp.float32) for weight in weights]
    if not first:
        accs = [
            acc + acc_in[begin:end, :] * jnp.concatenate([fade, fade], axis=1)
            for acc, fade, (begin, end) in zip(accs, fades, spans)
        ]
    if not last:
        top_out, acc_out = refs
        for acc, top, (begin, end) in zip(accs, tops, spans):
            top_out[begin:end, :] = top
            acc_out[begin:end, :] = acc
        return
    flow_hbm, matched_hbm, flow_ref, matched_ref, sems = refs
    copies = []
    for place, (acc, (begin, end)) in enumerate(zip(accs, spans)):
        inverse = 1.0 / acc[:, chans + 2 : chans + 3]
        matched_ref[begin:end, :] = (acc[:, :chans] * inverse).astype(jnp.bfloat16)
        copies.append(
            pltpu.make_async_copy(
                matched_ref.at[begin:end, :], matched_hbm.at[begin:end, :], sems.at[place]
            )
        )
        copies[-1].start()
        sums = jnp.transpose(acc[:, chans : chans + 8])
        sums = sums[:2, :] / sums[2:3, :]
        index = here * rows + begin + lax.broadcasted_iota(jnp.int32, (1, end - begin), 1)
        index = index.astype(jnp.float32)
        own_row = jnp.floor((index + 0.5) * (1.0 / W))
        own = jnp.concatenate([index - own_row * W, own_row], axis=0)
        flow_ref[:, begin:end] = (sums - own) * (1.0 / W)
    copies.append(pltpu.make_async_copy(flow_ref, flow_hbm, sems.at[len(spans)]))
    copies[-1].start()
    for copy in copies:
        copy.wait()


def fold(queries, positions, blocks, carry, last):
    rows, chans = queries.shape
    first = carry is None
    step = 128 if last else (rows // 2 + 127) // 128 * 128
    spans = [(begin, min(begin + step, rows)) for begin in range(0, rows, step)]
    operands = [queries, *[part for _, _, held in blocks for part in held], positions, *(carry or ())]
    keys = sum(held[0].shape[0] for _, _, held in blocks)
    if last:
        shapes = ((2, rows), jnp.float32), ((rows, chans), jnp.bfloat16)
        scratch = [pltpu.VMEM(shape, kind) for shape, kind in shapes]
        scratch.append(pltpu.SemaphoreType.DMA((len(spans) + 1,)))
    else:
        shapes = ((rows, chans), jnp.float32), ((rows, 2 * chans), jnp.float32)
        scratch = []
    return pl.pallas_call(
        functools.partial(fold_kernel, [(table, begin, len(held)) for table, begin, held in blocks], spans, first, last),
        out_shape=[jax.ShapeDtypeStruct(shape, kind) for shape, kind in shapes],
        in_specs=[VMEM] * len(operands),
        out_specs=[ANY if last else VMEM] * len(shapes),
        scratch_shapes=scratch,
        compiler_params=PARAMS,
        cost_estimate=pl.CostEstimate(
            flops=6 * rows * keys * chans, bytes_accessed=2 * keys * chans, transcendentals=rows * keys
        ),
    )(*operands)


def sources_of(targets):
    return [targets.index(z) for z in range(len(targets))]


def body(features):
    rows, chans = features.shape[2:]
    pix = lax.axis_size("pix")
    own = features.reshape(rows, chans)

    def send(array, targets, cross=True):
        return hop(array, targets, cross)

    positions = places(rows, chans)
    if pix == 4:
        cut = rows * 7 // 240 * 16
        x0 = send(own, [2, 0, 1, 3])
        x1 = send(own, [1, 2, 3, 0])
        x2 = send(own, [0, 3, 2, 1])
        relaya = send(x0[:cut], [1, 0, 3, 2], False)
        relayb = send(x0[cut:], [1, 0, 3, 2], False)
        groups = [
            [([1, 2, 0, 3], 0, [x0])],
            [([3, 0, 1, 2], 0, [x1])],
            [([0, 3, 2, 1], 0, [x2])],
            [([2, 1, 3, 0], 0, [relaya])],
            [([2, 1, 3, 0], cut, [relayb])],
        ]
    else:
        groups = []
        for shift in range(pix):
            targets = [(z + shift) % pix for z in range(pix)]
            groups.append([(sources_of(targets), 0, [send(own, targets)])])
    carry = None
    for place, blocks in enumerate(groups):
        carry = fold(own, positions, blocks, carry, place == len(groups) - 1)
    flow, matched = carry
    return flow.reshape(1, 1, 2, rows), matched.reshape(1, 1, rows, chans)


def solution(mesh):
    return jax.shard_map(
        body,
        mesh=mesh,
        in_specs=(P(("clips", "pair"), "dir", "pix", None),),
        out_specs=(
            P(("clips", "pair"), "dir", None, "pix"),
            P(("clips", "pair"), "dir", "pix", None),
        ),
        check_vma=False,
    )
```

```python
import functools
import math

import jax
import jax.numpy as jnp
from jax import lax
from jax.experimental import pallas as pl
from jax.experimental.pallas import tpu as pltpu
from jax.sharding import PartitionSpec as P

W = 120
VMEM = pl.BlockSpec(memory_space=pltpu.VMEM)
ANY = pl.BlockSpec(memory_space=pl.ANY)
PARAMS = pltpu.CompilerParams(vmem_limit_bytes=24 * 1024 * 1024)


def hop(array, targets, cross):
    frames = lax.axis_size("dir")
    flip = 1 if cross else 0
    pairs = [
        (z * frames + d, t * frames + (d ^ flip))
        for z, t in enumerate(targets)
        if t is not None
        for d in range(frames)
    ]
    return lax.ppermute(array, ("pix", "dir"), pairs)


def pick(table):
    here = lax.axis_index("pix")
    value = jnp.int32(0)
    for z, entry in enumerate(table):
        value = jnp.where(here == z, entry, value)
    return value


def places_kernel(out_ref):
    rows, chans = out_ref.shape
    column = lax.broadcasted_iota(jnp.int32, (rows, chans), 1)
    index = lax.broadcasted_iota(jnp.int32, (rows, chans), 0).astype(jnp.float32)
    row = jnp.floor((index + 0.5) * (1.0 / W))
    place = index - row * W
    values = jnp.where(column == 0, place, jnp.where(column == 1, row, 1.0))
    out_ref[...] = jnp.where(column < 3, values, 0.0).astype(jnp.bfloat16)


def places(rows, chans):
    return pl.pallas_call(
        places_kernel,
        out_shape=jax.ShapeDtypeStruct((rows, chans), jnp.bfloat16),
        out_specs=VMEM,
        compiler_params=PARAMS,
        cost_estimate=pl.CostEstimate(flops=rows * chans, bytes_accessed=0, transcendentals=0),
    )()


def fold_kernel(blocks, spans, first, last, *refs):
    refs = list(refs)
    q_ref = refs.pop(0)
    key_refs = [[refs.pop(0) for _ in range(n)] for _, _, n in blocks]
    places_ref = refs.pop(0)
    if not first:
        top_in, acc_in = refs.pop(0), refs.pop(0)
    rows, chans = q_ref.shape
    scale = chans ** (-0.5) * math.log2(math.e)
    here = lax.axis_index("pix")
    column = lax.broadcasted_iota(jnp.int32, (1, chans), 1)
    keys, values = [], []
    for (table, begin, _), held in zip(blocks, key_refs):
        part = held[0][...]
        if len(held) > 1:
            part = jnp.where((here == 0) | (here == len(table) - 1), held[1][...], part)
        start_row = pick(table) * (rows // W)
        offset = jnp.where(column == 1, start_row, 0).astype(jnp.float32).astype(jnp.bfloat16)
        keys.append(part)
        place = places_ref[begin : begin + part.shape[0], :]
        values.append(jnp.concatenate([part, place + offset], axis=1))
    keys = jnp.concatenate(keys, axis=0) if len(keys) > 1 else keys[0]
    values = jnp.concatenate(values, axis=0) if len(values) > 1 else values[0]
    count = keys.shape[0]
    scores = [
        lax.dot_general(
            q_ref[begin:end, :], keys, (((1,), (1,)), ((), ())), preferred_element_type=jnp.float32
        )
        for begin, end in spans
    ]
    tops, fades, weights = [], [], []
    for score, (begin, end) in zip(scores, spans):
        top = jnp.broadcast_to(jnp.max(score, axis=1, keepdims=True), (end - begin, chans))
        if not first:
            old = top_in[begin:end, :]
            top = jnp.maximum(old, top)
            fades.append(jnp.exp2((old - top) * scale))
        tops.append(top)
        parts = [
            jnp.exp2((score[:, j : j + chans] - top[:, : min(chans, count - j)]) * scale).astype(jnp.bfloat16)
            for j in range(0, count, chans)
        ]
        weights.append(jnp.concatenate(parts, axis=1) if len(parts) > 1 else parts[0])
    accs = [jnp.dot(weight, values, preferred_element_type=jnp.float32) for weight in weights]
    if not first:
        accs = [
            acc + acc_in[begin:end, :] * jnp.concatenate([fade, fade], axis=1)
            for acc, fade, (begin, end) in zip(accs, fades, spans)
        ]
    if not last:
        top_out, acc_out = refs
        for acc, top, (begin, end) in zip(accs, tops, spans):
            top_out[begin:end, :] = top
            acc_out[begin:end, :] = acc
        return
    flow_hbm, matched_hbm, flow_ref, matched_ref, sems = refs
    copies = []
    for place, (acc, (begin, end)) in enumerate(zip(accs, spans)):
        inverse = 1.0 / acc[:, chans + 2 : chans + 3]
        matched_ref[begin:end, :] = (acc[:, :chans] * inverse).astype(jnp.bfloat16)
        copies.append(
            pltpu.make_async_copy(
                matched_ref.at[begin:end, :], matched_hbm.at[begin:end, :], sems.at[place]
            )
        )
        copies[-1].start()
        sums = jnp.transpose(acc[:, chans:] * inverse)[:2, :]
        index = here * rows + begin + lax.broadcasted_iota(jnp.int32, (1, end - begin), 1)
        index = index.astype(jnp.float32)
        own_row = jnp.floor((index + 0.5) * (1.0 / W))
        own = jnp.concatenate([index - own_row * W, own_row], axis=0)
        flow_ref[:, begin:end] = (sums - own) * (1.0 / W)
    copies.append(pltpu.make_async_copy(flow_ref, flow_hbm, sems.at[len(spans)]))
    copies[-1].start()
    for copy in copies:
        copy.wait()


def fold(queries, positions, blocks, carry, last):
    rows, chans = queries.shape
    first = carry is None
    step = 128 if last else (rows // 2 + 127) // 128 * 128
    spans = [(begin, min(begin + step, rows)) for begin in range(0, rows, step)]
    operands = [queries, *[part for _, _, held in blocks for part in held], positions, *(carry or ())]
    keys = sum(held[0].shape[0] for _, _, held in blocks)
    if last:
        shapes = ((2, rows), jnp.float32), ((rows, chans), jnp.bfloat16)
        scratch = [pltpu.VMEM(shape, kind) for shape, kind in shapes]
        scratch.append(pltpu.SemaphoreType.DMA((len(spans) + 1,)))
    else:
        shapes = ((rows, chans), jnp.float32), ((rows, 2 * chans), jnp.float32)
        scratch = []
    return pl.pallas_call(
        functools.partial(fold_kernel, [(table, begin, len(held)) for table, begin, held in blocks], spans, first, last),
        out_shape=[jax.ShapeDtypeStruct(shape, kind) for shape, kind in shapes],
        in_specs=[VMEM] * len(operands),
        out_specs=[ANY if last else VMEM] * len(shapes),
        scratch_shapes=scratch,
        compiler_params=PARAMS,
        cost_estimate=pl.CostEstimate(
            flops=6 * rows * keys * chans, bytes_accessed=2 * keys * chans, transcendentals=rows * keys
        ),
    )(*operands)


def sources_of(targets):
    return [targets.index(z) for z in range(len(targets))]


def body(features):
    rows, chans = features.shape[2:]
    pix = lax.axis_size("pix")
    own = features.reshape(rows, chans)

    def send(array, targets, cross=True):
        return hop(array, targets, cross)

    positions = places(rows, chans)
    if pix == 4:
        cut = rows * 8 // 240 * 16
        x0 = send(own, [2, 0, 1, 3])
        x1 = send(own, [1, 2, 3, 0])
        x2 = send(own, [0, 3, 2, 1])
        relaya = send(x0[:cut], [1, 0, 3, 2], False)
        relayb = send(x0[cut:], [1, 0, 3, 2], False)
        groups = [
            [([1, 2, 0, 3], 0, [x0])],
            [([3, 0, 1, 2], 0, [x1])],
            [([0, 3, 2, 1], 0, [x2])],
            [([2, 1, 3, 0], 0, [relaya])],
            [([2, 1, 3, 0], cut, [relayb])],
        ]
    else:
        groups = []
        for shift in range(pix):
            targets = [(z + shift) % pix for z in range(pix)]
            groups.append([(sources_of(targets), 0, [send(own, targets)])])
    carry = None
    for place, blocks in enumerate(groups):
        carry = fold(own, positions, blocks, carry, place == len(groups) - 1)
    flow, matched = carry
    return flow.reshape(1, 1, 2, rows), matched.reshape(1, 1, rows, chans)


def solution(mesh):
    return jax.shard_map(
        body,
        mesh=mesh,
        in_specs=(P(("clips", "pair"), "dir", "pix", None),),
        out_specs=(
            P(("clips", "pair"), "dir", None, "pix"),
            P(("clips", "pair"), "dir", "pix", None),
        ),
        check_vma=False,
    )
```
